32 devices in a mesh: gx: 4 (over y, core), gy: 8 (over z, x).
Axes of the slice: x: 2, y: 2, z: 4, core: 2. Of those that a mesh axis runs over, the one named last changes fastest.
Arguments:
- macro_state: float32 [4, 512, 512], P(None, 'gx', 'gy'), may hold values from -6 to 6
- face_list: int32 [4, 8, 256], P('gx', 'gy'), may hold values from -1 to 16383, as said below
- owner: int32 [4, 8, 256, 1], P('gx', 'gy'), may hold values from 0 to 31; in each aligned block of 256 rows (0 to 255, 256 to 511, ..., all dimensions but the last counted through in order) at most 8 rows name the same one
- face_states: bfloat16 [4, 8, 256, 192, 128], P('gx', 'gy'), may hold values from -6 to 6
- micro_weight: bfloat16 [128, 128], replicated, may hold values from -0.5 to 0.5
- lift_weight: float32 [8, 128], replicated, may hold values from -2 to 2
- readout: float32 [128, 4], replicated, may hold values from -0.5 to 0.5
Outputs:
- macro_next: float32 [4, 512, 512], P(None, 'gx', 'gy')
- micro_states: bfloat16 [4, 8, 32, 8, 192, 128], P('gx', 'gy')
The draws below stay inside these ranges and needn't reach their ends.
Inputs may be any that keep to these rules, and one draw needn't show every extreme that they name: `face_list`: each tile lists distinct ids of its own faces (id = direction * 128 * 64 + i * 64 + j, as in the reference program), live entries first, then -1; every tile has 192 to 256 live slots, and some tile has 256. `owner`: among the 256 slots of one tile, live or empty, no ensemble device is named more than 8 times.
All inputs are finite; a program needn't handle non-finite values.
Results may differ from the reference program's by a relative error of at most 0.007.
Values may be sent and summed in bfloat16 or wider, within the bound.
No kernel may reach another device: no remote copies, remote signals or barrier semaphores. Data moves between devices by JAX's collectives and lax.ppermute only.
A program may use at most 128 MiB of HBM per device.

```python
import math
import jax
import jax.numpy as jnp
import numpy as np
from jax import lax

CX = 128
CY = 64
FMAX = 256
ENS = 192
S = 128
STEPS = 3
CAP = 8
NX = 512
NY = 512
N_GX = 4
N_GY = 8
DEVICES = 32


def draw_face_list(key, part):
    tile_total = N_GX * N_GY
    face_total = 2 * CX * CY
    tile_keys = jax.random.split(key, tile_total)
    shuffled = jax.vmap(lambda single: jax.random.permutation(single, face_total)[:FMAX])(tile_keys)
    counts = jax.random.randint(jax.random.fold_in(key, 11), (tile_total,), 3 * FMAX // 4, FMAX + 1)
    full_tile = jax.random.randint(jax.random.fold_in(key, 12), (), 0, tile_total)
    counts = jnp.where(jnp.arange(tile_total) == full_tile, FMAX, counts)
    positions = jnp.arange(FMAX)[None, :]
    listed = jnp.where(positions < counts[:, None], shuffled, -1)
    return listed.reshape(N_GX, N_GY, FMAX).astype(jnp.int32)


def levels(stream_key, shape, cuts, smallest, high):
    def one(dim, blocks):
        draws = jax.random.uniform(jax.random.fold_in(jax.random.fold_in(stream_key, 6), dim), (blocks,), jnp.float32, smallest / len(cuts), high / len(cuts))
        return jnp.repeat(jnp.exp(draws), shape[dim] // blocks).reshape((-1,) + (1,) * (len(shape) - dim - 1))

    factor_of = one(*cuts[0])
    for cut in cuts[1:]:
        factor_of = factor_of * one(*cut)
    return factor_of


def routed_block(rng, own, number, rows, number_of, top, reach, lean):
    order = jax.random.permutation(rng, number_of)
    crowded, ordinary = shares(number_of, rows * top, reach, lean, True), shares(number_of, rows * top, reach, lean, False)
    places = jnp.arange(number_of)

    def named(sizes, turn):
        used = int((sizes > 0).sum())
        fixed = max(1, used // 4)
        passed = fixed + (places - fixed + turn * (used - fixed)) % max(1, number_of - fixed)
        return jnp.zeros((number_of,), jnp.int32).at[order[jnp.where(places < fixed, places, passed)]].set(jnp.asarray(sizes, jnp.int32))

    sizes = jnp.where(number % 4 == 0, named(crowded, number // 4), named(ordinary, number - number // 4 - 1))
    mixed = jax.random.permutation(jax.random.fold_in(own, 3), number_of)
    donor, receiver = mixed[0:number_of // 2 * 2:2], mixed[1:number_of // 2 * 2:2]
    slack = jnp.minimum(sizes[donor] - 1, reach - sizes[receiver]) // 2
    slack = jnp.where((donor == order[0]) | (receiver == order[0]) | (sizes[receiver] == 0), 0, jnp.maximum(slack, 0))
    passed = jax.random.randint(jax.random.fold_in(own, 4), (number_of // 2,), 0, 1 << 20) % (slack + 1)
    sizes = sizes.at[donor].add(-passed).at[receiver].add(passed)
    items = jnp.searchsorted(jnp.cumsum(sizes), jnp.arange(rows * top), side="right").astype(jnp.int32)
    grid = items.reshape(top, rows).T
    grid = grid[jax.random.permutation(jax.random.fold_in(own, 1), rows)]
    turn = jax.random.randint(jax.random.fold_in(own, 2), (rows, 1), 0, top)
    return jnp.take_along_axis(grid, (jnp.arange(top)[None, :] + turn) % top, axis=1)


def shares(count, total, most, skew, full):
    portions = [(1 << 20) // math.isqrt(standing ** skew) + 1 for standing in range(1, count + 1)]
    largest = most if full else min(most, max(-(-total // count), total * portions[0] // sum(portions)))
    least = 1 if total - largest >= count - 1 else 0
    holding, surplus = [largest] + [least] * (count - 1), total - largest - least * (count - 1)
    while surplus > 0:
        movable = [i for i in range(1, count) if holding[i] < largest] or [i for i in range(1, count) if holding[i] < most]
        pool, left = sum([portions[i] for i in movable]), surplus
        for i in movable:
            more = min(most - holding[i], max(1, left * portions[i] // pool), surplus)
            holding[i] = holding[i] + more
            surplus = surplus - more
    return np.array(holding)


def noise(stream_key, dims, width, limit, cuts=(), kind=jnp.bfloat16):
    entries = width * jax.random.normal(stream_key, dims, jnp.float32)
    if cuts:
        entries = entries * levels(stream_key, dims, cuts, -0.22, 0.18)
    return jnp.clip(entries, -limit, limit).astype(kind)


def setup_inputs(seed: int = 0) -> dict:
    splits = jax.random.split(jax.random.key(seed), 8)
    macro_state = noise(splits[0], (4, NX, NY), 1.0, 6.0, ((1, 4), (2, 8)), jnp.float32)
    face_list = draw_face_list(jax.random.fold_in(splits[7], 71), 0)
    owner_keys = jax.random.split(jax.random.fold_in(splits[2], 1), N_GX * N_GY * FMAX // FMAX)
    owner_turns = jax.random.permutation(jax.random.fold_in(splits[2], 3), N_GX * N_GY * FMAX // FMAX)
    owner = jax.vmap(lambda own, number: routed_block(jax.random.fold_in(splits[2], 2), own, number, FMAX, DEVICES, 1, CAP, 2))(owner_keys, owner_turns).reshape((N_GX, N_GY, FMAX, 1))
    face_states = noise(splits[3], (N_GX, N_GY, FMAX, ENS, S), 1.0, 6.0, ((0, 4), (1, 8)))
    micro_weight = noise(splits[4], (S, S), S ** -0.5, 0.5)
    lift_weight = noise(splits[5], (8, S), 8 ** -0.5, 2.0, (), jnp.float32)
    readout = noise(splits[6], (S, 4), S ** -0.5, 0.5, (), jnp.float32)
    return {"macro_state": macro_state, "face_list": face_list, "owner": owner, "face_states": face_states, "micro_weight": micro_weight, "lift_weight": lift_weight, "readout": readout}


diffusion = 0.2
relax_rate = 0.5
time_step = 0.5


def relax_faces(states, inputs, micro_weight, lift_weight, readout):
    leading = states.shape[:-2]
    members = states.shape[-2]
    state_width = states.shape[-1]
    slot_count = math.prod(leading)
    current = states.reshape(slot_count, members, state_width)
    slot_inputs = inputs.reshape(slot_count, inputs.shape[-1])
    forcing = jnp.dot(slot_inputs[:, :8], lift_weight, precision=lax.Precision.HIGHEST)
    live_mask = slot_inputs[:, 8]
    group_size = math.gcd(slot_count, 32)
    groups = slot_count // group_size

    def advance(block_data):
        block_states, block_force, block_live = block_data
        for repeat in range(STEPS):
            flat_rows = block_states.reshape(group_size * members, state_width)
            activation = jnp.dot(flat_rows, micro_weight, preferred_element_type=jnp.float32)
            activation = activation.reshape(group_size, members, state_width)
            block_states = ((1.0 - relax_rate) * block_states.astype(jnp.float32)
                            + relax_rate * jnp.tanh(activation + block_force[:, None, :])).astype(jnp.bfloat16)
        block_states = block_states * block_live[:, None, None].astype(jnp.bfloat16)
        ensemble_mean = jnp.sum(block_states, axis=1, dtype=jnp.float32) / members
        face_flux = jnp.dot(ensemble_mean, readout, precision=lax.Precision.HIGHEST)
        return block_states, face_flux

    relaxed, face_flux = lax.map(advance, (current.reshape(groups, group_size, members, state_width),
                                           forcing.reshape(groups, group_size, state_width),
                                           live_mask.reshape(groups, group_size)))
    return relaxed.reshape(states.shape), face_flux.reshape(leading + (readout.shape[1],))


def reference(macro_state, face_list, owner, face_states, micro_weight, lift_weight, readout):
    tile_total = N_GX * N_GY
    face_ids = face_list.reshape(tile_total, FMAX)
    live = face_ids >= 0
    safe_index = jnp.where(live, face_ids, 0)
    tile_ids = jnp.arange(tile_total, dtype=jnp.int32)
    tile_row = tile_ids // N_GY
    tile_col = tile_ids % N_GY
    direction = safe_index // (CX * CY)
    cell_index = safe_index % (CX * CY)
    global_row = tile_row[:, None] * CX + cell_index // CY
    global_col = tile_col[:, None] * CY + cell_index % CY
    right_row = jnp.where(direction == 1, (global_row + 1) % NX, global_row)
    right_col = jnp.where(direction == 0, (global_col + 1) % NY, global_col)
    left_vals = macro_state[:, global_row, global_col]
    right_vals = macro_state[:, right_row, right_col]
    inputs = jnp.concatenate([jnp.transpose(left_vals, (1, 2, 0)), jnp.transpose(right_vals, (1, 2, 0)),
                              live[..., None].astype(jnp.float32)], axis=-1)

    def per_tile(pieces):
        return relax_faces(pieces[0], pieces[1], micro_weight, lift_weight, readout)

    relaxed, face_flux = lax.map(per_tile, (face_states.reshape(tile_total, FMAX, ENS, S), inputs))
    destination = owner.reshape(tile_total, FMAX)
    onehot = (destination[..., None] == jnp.arange(DEVICES, dtype=jnp.int32)).astype(jnp.int32)
    slot_rank = jnp.sum((jnp.cumsum(onehot, axis=1) - onehot) * onehot, axis=-1).astype(jnp.int32)
    gathered = jnp.zeros((DEVICES, tile_total, CAP, ENS, S), jnp.bfloat16)
    gathered = gathered.at[destination, jnp.broadcast_to(tile_ids[:, None], destination.shape), slot_rank].set(relaxed)
    micro_states = gathered.reshape(N_GX, N_GY, DEVICES, CAP, ENS, S)

    east_flux = diffusion * (macro_state - jnp.roll(macro_state, -1, axis=2))
    south_flux = diffusion * (macro_state - jnp.roll(macro_state, -1, axis=1))
    face_values = jnp.stack([east_flux, south_flux], axis=1)
    drop_row = jnp.where(live, global_row, NX)
    face_values = face_values.at[:, direction, drop_row, global_col].set(
        jnp.transpose(face_flux, (2, 0, 1)), mode="drop")
    east_flux = face_values[:, 0]
    south_flux = face_values[:, 1]
    macro_next = macro_state - time_step * (east_flux - jnp.roll(east_flux, 1, axis=2)
                                            + south_flux - jnp.roll(south_flux, 1, axis=1))
    return macro_next, micro_states
```

```python
import functools

import jax
import jax.numpy as jnp
from jax import lax
from jax.experimental import pallas as pl
from jax.experimental.pallas import tpu as pltpu
from jax.sharding import PartitionSpec as P


STEPS = 3
RAW = 2
GROUP = 4


diffusion = 0.2
relax_rate = 0.5
time_step = 0.5
HIGHEST = lax.Precision.HIGHEST


def passed_along(value, axis, steps):
    count = lax.axis_size(axis)
    pairs = [(source, (source + steps) % count) for source in range(count)]
    return lax.ppermute(value, axis, pairs)


def partner_order(gx_count, gy_count):
    devices = gx_count * gy_count
    far = [k for k in range(1, devices) if k & (gy_count // 2)]
    near = [k for k in range(1, devices) if not k & (gy_count // 2)]
    order, taken = list(far[:2]), 0
    for place, k in enumerate(far[2:]):
        order.append(k)
        want = (place + 1) * len(near) // max(1, len(far) - 4)
        while taken < min(want, len(near)):
            order.append(near[taken])
            taken += 1
    return order + near[taken:]


def partner_groups(order):
    todo = order[RAW:] + order[:RAW] + [0]
    return [todo[:2]] + [todo[i : i + GROUP] for i in range(2, len(todo), GROUP)]


def route_kernel(capacity, raw, me_ref, owner_ref, face_ref, states_ref, table_ref, ids_ref, *rest):
    out_refs, (count_ref, buffer, in_sem, out_sem) = rest[: len(raw)], rest[len(raw) :]
    slot_total = owner_ref.shape[0]
    me = me_ref[0]

    def clear(number, carry):
        count_ref[number] = 0
        return carry

    lax.fori_loop(0, count_ref.shape[0], clear, 0)

    def place(slot, carry):
        code = jnp.bitwise_xor(owner_ref[slot], me)
        rank = count_ref[code]
        count_ref[code] = rank + 1
        position = code * capacity + rank
        table_ref[position] = slot
        ids_ref[position] = face_ref[slot]
        return carry

    lax.fori_loop(0, slot_total, place, 0, unroll=8)

    def fetch(turn, i):
        slot = table_ref[raw[turn] * capacity + i]
        return pltpu.make_async_copy(states_ref.at[slot], buffer.at[turn, i], in_sem.at[turn, i])

    def send(turn, i):
        return pltpu.make_async_copy(buffer.at[turn, i], out_refs[turn].at[i], out_sem.at[turn, i])

    steps = [(turn, i) for turn in range(len(raw)) for i in range(capacity)]
    for step in steps:
        fetch(*step).start()
    for step in steps:
        fetch(*step).wait()
        send(*step).start()
    for step in steps:
        send(*step).wait()


def forcing_kernel(capacity, raw, macro_ref, row_ref, col_ref, place_ref, lift_ref, force_ref, live_ref, *out_refs):
    channels, tile_rows, tile_cols = macro_ref.shape
    slot_total = place_ref.shape[0]
    place = place_ref[...]
    left_row, left_col, right_row, right_col, live = [place[:, i : i + 1] for i in range(5)]
    row_iota = lax.broadcasted_iota(jnp.int32, (slot_total, tile_rows), 1)
    col_iota = lax.broadcasted_iota(jnp.int32, (slot_total, tile_cols), 1)
    left_pick = (row_iota == left_row).astype(jnp.float32)
    right_pick = (row_iota == right_row).astype(jnp.float32)
    left_mask = col_iota == left_col
    right_mask = col_iota == right_col
    edge_row = right_mask & (right_row == tile_rows)
    edge_col = (row_iota == right_row) & (right_col == tile_cols)
    total = jnp.zeros((slot_total, lift_ref.shape[1]), jnp.float32)
    for channel in range(channels):
        block = macro_ref[channel]
        left = jnp.dot(left_pick, block, precision=HIGHEST, preferred_element_type=jnp.float32)
        left = jnp.sum(jnp.where(left_mask, left, 0.0), axis=1, keepdims=True)
        right = jnp.dot(right_pick, block, precision=HIGHEST, preferred_element_type=jnp.float32)
        right = jnp.where(right_mask, right, 0.0) + jnp.where(edge_row, row_ref[channel : channel + 1, :], 0.0)
        right = jnp.sum(right, axis=1, keepdims=True)
        beyond = jnp.where(edge_col, col_ref[channel : channel + 1, :], 0.0)
        right = right + jnp.sum(beyond, axis=1, keepdims=True)
        total = total + left * lift_ref[channel : channel + 1, :]
        total = total + right * lift_ref[channels + channel : channels + channel + 1, :]
    force_ref[...] = total
    alive = jnp.broadcast_to((live > 0).astype(jnp.float32), total.shape)
    live_ref[...] = alive
    for turn, k in enumerate(raw):
        out_refs[turn][0:capacity, :] = total[k * capacity : (k + 1) * capacity, :]
        out_refs[turn][capacity:, :] = alive[k * capacity : (k + 1) * capacity, :]


def relaxed_states(current, force, weight, live):
    slots, members, width = current.shape
    force = force.reshape(slots, 1, width)
    for _ in range(STEPS):
        activation = jnp.dot(current.reshape(slots * members, width), weight, preferred_element_type=jnp.float32)
        activation = activation.reshape(slots, members, width) + force
        current = (
            (1.0 - relax_rate) * current.astype(jnp.float32) + relax_rate * jnp.tanh(activation)
        ).astype(jnp.bfloat16)
    return current * live.astype(jnp.bfloat16).reshape(slots, 1, width)


def relax_kernel(
    capacity, partners, kept, own, me_ref, table_ref, states_ref, force_ref, live_ref, weight_ref, *rest
):
    out_refs, (sums_ref, in_buffer, out_buffer, in_sem, out_sem) = rest[: len(kept)], rest[len(kept) :]
    target = {k: ref for k, ref in zip(kept, out_refs)}

    def fetch(turn, i):
        slot = table_ref[partners[turn] * capacity + i]
        return pltpu.make_async_copy(states_ref.at[slot], in_buffer.at[turn % 2, i], in_sem.at[turn % 2, i])

    def send(turn):
        k = partners[turn]
        ref = target[k].at[me_ref[0]] if k == own else target[k]
        return pltpu.make_async_copy(out_buffer.at[turn % 2], ref, out_sem.at[turn % 2])

    for i in range(capacity):
        fetch(0, i).start()
    weight = weight_ref[...]
    waiting = {}
    for turn, k in enumerate(partners):
        if turn + 1 < len(partners):
            for i in range(capacity):
                fetch(turn + 1, i).start()
        if turn % 2 in waiting:
            send(waiting.pop(turn % 2)).wait()
        for i in range(capacity):
            fetch(turn, i).wait()

        rows = slice(k * capacity, (k + 1) * capacity)
        block = relaxed_states(in_buffer[turn % 2], force_ref[rows, :], weight, live_ref[rows, :])
        out_buffer[turn % 2] = block
        sums_ref[turn * capacity : (turn + 1) * capacity, :] = jnp.sum(block.astype(jnp.float32), axis=1)
        if k in target:
            send(turn).start()
            waiting[turn % 2] = turn
    for turn in waiting.values():
        send(turn).wait()


def land_kernel(capacity, source_ref, raw_ref, force_ref, weight_ref, whole_ref, out_ref, buffer, out_sem):
    buffer[...] = relaxed_states(
        raw_ref[...], force_ref[0:capacity, :], weight_ref[...], force_ref[capacity:, :]
    )
    copy = pltpu.make_async_copy(buffer, out_ref.at[source_ref[0]], out_sem)
    copy.start()
    copy.wait()


def flux_kernel(members, sums_ref, readout_ref, place_ref, place_row_ref, flux_ref, hit_ref):
    _, channels, tile_rows, tile_cols = flux_ref.shape
    slot_total = place_ref.shape[0]
    mean = sums_ref[...] / members
    flux = jnp.dot(mean, readout_ref[...], precision=HIGHEST, preferred_element_type=jnp.float32)
    col_iota = lax.broadcasted_iota(jnp.int32, (slot_total, tile_cols), 1)
    col_pick = (col_iota == place_ref[:, 1:2]).astype(jnp.float32)
    row_iota = lax.broadcasted_iota(jnp.int32, (tile_rows, slot_total), 0)
    row_pick = (row_iota == place_row_ref[0:1, :]) & (place_row_ref[4:5, :] > 0)
    for direction in range(2):
        pick = (row_pick & (place_row_ref[5:6, :] == direction)).astype(jnp.float32)
        hit_ref[direction] = jnp.dot(pick, col_pick, precision=HIGHEST, preferred_element_type=jnp.float32)
        for channel in range(channels):
            spread = col_pick * flux[:, channel : channel + 1]
            flux_ref[direction, channel] = jnp.dot(
                pick, spread, precision=HIGHEST, preferred_element_type=jnp.float32
            )


ANY = pl.BlockSpec(memory_space=pl.ANY)
VMEM = pl.BlockSpec(memory_space=pltpu.VMEM)
SMEM = pl.BlockSpec(memory_space=pltpu.SMEM)


def per_device(macro_state, face_list, owner, face_states, micro_weight, lift_weight, readout):
    channels, tile_rows, tile_cols = macro_state.shape
    slot_total = face_list.shape[2]
    members, state_width = face_states.shape[3:]
    gx_count, gy_count = lax.axis_size("gx"), lax.axis_size("gy")
    devices = gx_count * gy_count
    capacity = max(2, slot_total // devices)
    assert capacity * devices == slot_total and devices & (devices - 1) == 0
    order = partner_order(gx_count, gy_count)
    raw = order[:RAW]
    block = jax.ShapeDtypeStruct((capacity, members, state_width), jnp.bfloat16)
    whole = jax.ShapeDtypeStruct((devices, capacity, members, state_width), jnp.bfloat16)
    me = lax.axis_index("gx") * gy_count + lax.axis_index("gy")
    me_ref = me.astype(jnp.int32).reshape(1)
    states = face_states.reshape(slot_total, members, state_width)
    faces = face_list.reshape(slot_total)

    def exchanged(value, k):
        return lax.ppermute(value, ("gx", "gy"), [(source, source ^ k) for source in range(devices)])

    slots_smem = jax.ShapeDtypeStruct((slot_total,), jnp.int32)
    table, ids, *raw_sent = pl.pallas_call(
        functools.partial(route_kernel, capacity, raw),
        out_shape=[slots_smem, slots_smem] + [block] * len(raw),
        in_specs=[SMEM, SMEM, SMEM, ANY],
        out_specs=[SMEM, SMEM] + [ANY] * len(raw),
        scratch_shapes=[
            pltpu.SMEM((devices,), jnp.int32),
            pltpu.VMEM((len(raw), capacity, members, state_width), jnp.bfloat16),
            pltpu.SemaphoreType.DMA((len(raw), capacity)),
            pltpu.SemaphoreType.DMA((len(raw), capacity)),
        ],
        name="route",
    )(me_ref, owner.reshape(slot_total), faces, states)

    raw_got = []
    for turn, k in enumerate(raw):
        raw_got.append(exchanged(raw_sent[turn], k))

    first_row, first_col, table = lax.optimization_barrier((macro_state[:, 0, :], macro_state[:, :, 0], table))
    next_row = passed_along(first_row, "gx", -1)
    next_col = passed_along(first_col, "gy", -1)

    live = ids >= 0
    safe = jnp.where(live, ids, 0)
    direction = safe // (tile_rows * tile_cols)
    cell = safe % (tile_rows * tile_cols)
    left_row, left_col = cell // tile_cols, cell % tile_cols
    right_row, right_col = left_row + direction, left_col + 1 - direction
    place = [left_row, left_col, right_row, right_col, live.astype(jnp.int32), direction, cell, safe]
    place_rows = jnp.stack(place, axis=0)
    place_cols = jnp.stack(place, axis=1)

    force, alive, *raw_force = pl.pallas_call(
        functools.partial(forcing_kernel, capacity, raw),
        out_shape=[jax.ShapeDtypeStruct((slot_total, state_width), jnp.float32)] * 2
        + [jax.ShapeDtypeStruct((2 * capacity, state_width), jnp.float32)] * len(raw),
        in_specs=[VMEM] * 5,
        out_specs=[VMEM] * (2 + len(raw)),
        name="forcing",
    )(macro_state, next_row, next_col, place_cols, lift_weight)

    force_got = []
    for turn, k in enumerate(raw):
        force_got.append(exchanged(raw_force[turn], k))

    groups = partner_groups(order)
    sums, relaxed = {}, {}
    for partners in groups:
        kept = [k for k in partners if k not in raw]
        *blocks, part = pl.pallas_call(
            functools.partial(relax_kernel, capacity, partners, kept, 0),
            out_shape=[whole if k == 0 else block for k in kept]
            + [jax.ShapeDtypeStruct((len(partners) * capacity, state_width), jnp.float32)],
            in_specs=[SMEM, SMEM, ANY, VMEM, VMEM, VMEM],
            out_specs=[ANY] * len(kept) + [VMEM],
            scratch_shapes=[
                pltpu.VMEM((2, capacity, members, state_width), jnp.bfloat16),
                pltpu.VMEM((2, capacity, members, state_width), jnp.bfloat16),
                pltpu.SemaphoreType.DMA((2, capacity)),
                pltpu.SemaphoreType.DMA((2,)),
            ],
        )(me_ref, table, states, force, alive, micro_weight)
        table, part = lax.optimization_barrier((table, part))
        for k, value in zip(kept, blocks):
            relaxed[k] = value
        for turn, k in enumerate(partners):
            sums[k] = part[turn * capacity : (turn + 1) * capacity]
    all_sums = jnp.concatenate([sums[k] for k in range(devices)], axis=0)

    got = {}
    for k in order[RAW:]:
        got[k] = exchanged(relaxed[k], k)

    face_flux, hit = pl.pallas_call(
        functools.partial(flux_kernel, members),
        out_shape=[
            jax.ShapeDtypeStruct((2, channels, tile_rows, tile_cols), jnp.float32),
            jax.ShapeDtypeStruct((2, tile_rows, tile_cols), jnp.float32),
        ],
        in_specs=[VMEM] * 4,
        out_specs=[VMEM] * 2,
        name="flux",
    )(all_sums, readout, place_cols, place_rows)
    beyond_row = jnp.concatenate([macro_state[:, 1:, :], next_row[:, None, :]], axis=1)
    beyond_col = jnp.concatenate([macro_state[:, :, 1:], next_col[:, :, None]], axis=2)
    east_flux = jnp.where(hit[0] > 0.5, face_flux[0], diffusion * (macro_state - beyond_col))
    south_flux = jnp.where(hit[1] > 0.5, face_flux[1], diffusion * (macro_state - beyond_row))
    west_flux = passed_along(east_flux[:, :, -1], "gy", 1)
    north_flux = passed_along(south_flux[:, -1, :], "gx", 1)
    macro_next = macro_state - time_step * (
        east_flux
        - jnp.concatenate([west_flux[:, :, None], east_flux[:, :, :-1]], axis=2)
        + south_flux
        - jnp.concatenate([north_flux[:, None, :], south_flux[:, :-1, :]], axis=1)
    )

    out = relaxed[0]
    for turn, k in enumerate(raw):
        out = pl.pallas_call(
            functools.partial(land_kernel, capacity),
            out_shape=whole,
            in_specs=[SMEM, VMEM, VMEM, VMEM, ANY],
            out_specs=ANY,
            scratch_shapes=[
                pltpu.VMEM((capacity, members, state_width), jnp.bfloat16),
                pltpu.SemaphoreType.DMA,
            ],
            input_output_aliases={4: 0},
        )(jnp.bitwise_xor(me_ref, k), raw_got[turn], force_got[turn], micro_weight, out)
    for k in order[RAW:]:
        out = lax.dynamic_update_slice(out, got[k][None], (jnp.bitwise_xor(me, k), 0, 0, 0))
    return macro_next, out.reshape(1, 1, devices, capacity, members, state_width)


def solution(mesh):
    return jax.shard_map(
        per_device,
        mesh=mesh,
        in_specs=(
            P(None, "gx", "gy"),
            P("gx", "gy", None),
            P("gx", "gy", None, None),
            P("gx", "gy", None, None, None),
            P(),
            P(),
            P(),
        ),
        out_specs=(P(None, "gx", "gy"), P("gx", "gy", None, None, None, None)),
        check_vma=False,
    )
```

```python
import functools

import jax
import jax.numpy as jnp
from jax import lax
from jax.experimental import pallas as pl
from jax.experimental.pallas import tpu as pltpu
from jax.sharding import PartitionSpec as P


STEPS = 3
RAW = 2
GROUP = 4


diffusion = 0.2
relax_rate = 0.5
time_step = 0.5
HIGHEST = lax.Precision.HIGHEST


def passed_along(value, axis, steps):
    count = lax.axis_size(axis)
    pairs = [(source, (source + steps) % count) for source in range(count)]
    return lax.ppermute(value, axis, pairs)


def partner_order(gx_count, gy_count):
    devices = gx_count * gy_count
    far_bit, row_bit, col_bit = gy_count // 2, 1, devices // 2
    turns = lambda k: (bool(k & (far_bit // 2)), bool(k & row_bit), bool(k & col_bit), k)
    far = sorted([k for k in range(1, devices) if k & far_bit], key=turns)
    near = [k for k in range(1, devices) if not k & far_bit]
    near.sort(key=lambda k: (not k & row_bit, not k & col_bit, k))
    order, spare = far[:RAW], max(0, len(near) - len(far) + RAW)
    for place, k in enumerate(far[RAW:]):
        take = 2 if place < spare else 1
        order += [k] + near[:take]
        near = near[take:]
    return order + near


def partner_groups(order):
    todo = order[RAW:] + order[:RAW] + [0]
    return [todo[:2]] + [todo[i : i + GROUP] for i in range(2, len(todo), GROUP)]


def block_copies(turns, capacity, slot_of, states_ref, out_refs, buffer, in_sem, out_sem, between=None):
    def fetch(turn, i):
        return pltpu.make_async_copy(states_ref.at[slot_of(turn, i)], buffer.at[turn, i], in_sem.at[turn, i])

    def send(turn, i):
        return pltpu.make_async_copy(buffer.at[turn, i], out_refs[turn].at[i], out_sem.at[turn, i])

    steps = [(turn, i) for turn in range(turns) for i in range(capacity)]
    for step in steps:
        fetch(*step).start()
    if between is not None:
        between()
    for step in steps:
        fetch(*step).wait()
        send(*step).start()
    for step in steps:
        send(*step).wait()


def first_kernel(capacity, partner, me_ref, owner_ref, macro_ref, states_ref, out_ref, row_ref, col_ref, *scratch):
    slot_ref, macro_buffer, macro_sem, *gather = scratch
    slot_total = owner_ref.shape[0]
    owner = jnp.bitwise_xor(me_ref[0], partner)
    fields = pltpu.make_async_copy(macro_ref, macro_buffer, macro_sem)
    fields.start()

    def look(slot, found):
        slot_ref[found] = slot
        return found + (owner_ref[slot] == owner).astype(jnp.int32)

    lax.fori_loop(0, slot_total, look, jnp.int32(0), unroll=8)

    def edges():
        fields.wait()
        channels, _, tile_rows = macro_buffer.shape
        pick = (lax.broadcasted_iota(jnp.int32, (8, tile_rows), 1) == 0).astype(jnp.float32)
        for channel in range(channels):
            field = macro_buffer[channel]
            col_ref[channel : channel + 1, :] = field[0:1, :]
            rows = lax.dot_general(
                pick, field, (((1,), (1,)), ((), ())), precision=HIGHEST, preferred_element_type=jnp.float32
            )
            row_ref[channel : channel + 1, :] = rows[0:1, :]

    block_copies(1, capacity, lambda turn, i: slot_ref[i], states_ref, [out_ref], *gather, between=edges)


def route_kernel(capacity, partners, me_ref, owner_ref, face_ref, states_ref, table_ref, ids_ref, *rest):
    out_refs, (count_ref, buffer, in_sem, out_sem) = rest[: len(partners)], rest[len(partners) :]
    slot_total = owner_ref.shape[0]
    me = me_ref[0]

    def clear(number, carry):
        count_ref[number] = 0
        return carry

    lax.fori_loop(0, count_ref.shape[0], clear, 0)

    def place(slot, carry):
        code = jnp.bitwise_xor(owner_ref[slot], me)
        rank = count_ref[code]
        count_ref[code] = rank + 1
        position = code * capacity + rank
        table_ref[position] = slot
        ids_ref[position] = face_ref[slot]
        return carry

    lax.fori_loop(0, slot_total, place, 0, unroll=8)
    slot_of = lambda turn, i: table_ref[partners[turn] * capacity + i]
    block_copies(len(partners), capacity, slot_of, states_ref, out_refs, buffer, in_sem, out_sem)


def forcing_kernel(
    capacity, raw, macro_ref, row_ref, col_ref, place_ref, lift_ref, force_ref, live_ref, *out_refs
):
    channels, tile_cols, tile_rows = macro_ref.shape
    slot_total = place_ref.shape[0]
    place = place_ref[...]
    left_row, left_col, right_row, right_col, live = [place[:, i : i + 1] for i in range(5)]
    row_iota = lax.broadcasted_iota(jnp.int32, (slot_total, tile_rows), 1)
    col_iota = lax.broadcasted_iota(jnp.int32, (slot_total, tile_cols), 1)
    left_pick = (col_iota == left_col).astype(jnp.float32)
    right_pick = (col_iota == right_col).astype(jnp.float32)
    left_mask = row_iota == left_row
    right_mask = row_iota == right_row
    edge_row = (col_iota == right_col) & (right_row == tile_rows)
    edge_col = right_mask & (right_col == tile_cols)
    total = jnp.zeros((slot_total, lift_ref.shape[1]), jnp.float32)
    for channel in range(channels):
        block = macro_ref[channel]
        left = jnp.dot(left_pick, block, precision=HIGHEST, preferred_element_type=jnp.float32)
        left = jnp.sum(jnp.where(left_mask, left, 0.0), axis=1, keepdims=True)
        right = jnp.dot(right_pick, block, precision=HIGHEST, preferred_element_type=jnp.float32)
        right = jnp.where(right_mask, right, 0.0) + jnp.where(edge_col, col_ref[channel : channel + 1, :], 0.0)
        right = jnp.sum(right, axis=1, keepdims=True)
        beyond = jnp.where(edge_row, row_ref[channel : channel + 1, :], 0.0)
        right = right + jnp.sum(beyond, axis=1, keepdims=True)
        total = total + left * lift_ref[channel : channel + 1, :]
        total = total + right * lift_ref[channels + channel : channels + channel + 1, :]
    force_ref[...] = total
    alive = jnp.broadcast_to((live > 0).astype(jnp.float32), total.shape)
    live_ref[...] = alive
    for turn, k in enumerate(raw):
        out_refs[turn][0:capacity, :] = total[k * capacity : (k + 1) * capacity, :]
        out_refs[turn][capacity:, :] = alive[k * capacity : (k + 1) * capacity, :]


def relaxed_states(current, force, weight, live):
    slots, members, width = current.shape
    force = force.reshape(slots, 1, width)
    for _ in range(STEPS):
        activation = jnp.dot(current.reshape(slots * members, width), weight, preferred_element_type=jnp.float32)
        activation = activation.reshape(slots, members, width) + force
        current = (
            (1.0 - relax_rate) * current.astype(jnp.float32) + relax_rate * jnp.tanh(activation)
        ).astype(jnp.bfloat16)
    return current * live.astype(jnp.bfloat16).reshape(slots, 1, width)


def relax_kernel(
    capacity, partners, kept, own, me_ref, table_ref, states_ref, force_ref, live_ref, weight_ref, *rest
):
    out_refs, (sums_ref, in_buffer, out_buffer, in_sem, out_sem) = rest[: len(kept)], rest[len(kept) :]
    target = {k: ref for k, ref in zip(kept, out_refs)}

    def fetch(turn, i):
        slot = table_ref[partners[turn] * capacity + i]
        return pltpu.make_async_copy(states_ref.at[slot], in_buffer.at[turn % 2, i], in_sem.at[turn % 2, i])

    def send(turn):
        k = partners[turn]
        ref = target[k].at[me_ref[0]] if k == own else target[k]
        return pltpu.make_async_copy(out_buffer.at[turn % 2], ref, out_sem.at[turn % 2])

    for i in range(capacity):
        fetch(0, i).start()
    weight = weight_ref[...]
    waiting = {}
    for turn, k in enumerate(partners):
        if turn + 1 < len(partners):
            for i in range(capacity):
                fetch(turn + 1, i).start()
        if turn % 2 in waiting:
            send(waiting.pop(turn % 2)).wait()
        for i in range(capacity):
            fetch(turn, i).wait()

        rows = slice(k * capacity, (k + 1) * capacity)
        block = relaxed_states(in_buffer[turn % 2], force_ref[rows, :], weight, live_ref[rows, :])
        out_buffer[turn % 2] = block
        sums_ref[turn * capacity : (turn + 1) * capacity, :] = jnp.sum(block.astype(jnp.float32), axis=1)
        if k in target:
            send(turn).start()
            waiting[turn % 2] = turn
    for turn in waiting.values():
        send(turn).wait()


def land_kernel(capacity, source_ref, raw_ref, force_ref, weight_ref, whole_ref, out_ref, buffer, out_sem):
    buffer[...] = relaxed_states(
        raw_ref[...], force_ref[0:capacity, :], weight_ref[...], force_ref[capacity:, :]
    )
    copy = pltpu.make_async_copy(buffer, out_ref.at[source_ref[0]], out_sem)
    copy.start()
    copy.wait()


def put_kernel(partners, me_ref, *rest):
    got_refs, (_, out_ref, buffer, in_sem, out_sem) = rest[: len(partners)], rest[len(partners) :]
    places = [jnp.bitwise_xor(me_ref[0], k) for k in partners]
    fetches = [pltpu.make_async_copy(got_refs[i], buffer.at[i], in_sem.at[i]) for i in range(len(partners))]
    sends = [
        pltpu.make_async_copy(buffer.at[i], out_ref.at[place], out_sem.at[i]) for i, place in enumerate(places)
    ]
    for fetch in fetches:
        fetch.start()
    for fetch, send in zip(fetches, sends):
        fetch.wait()
        send.start()
    for send in sends:
        send.wait()


def flux_kernel(members, sums_ref, readout_ref, place_ref, place_row_ref, flux_ref, hit_ref):
    _, channels, tile_rows, tile_cols = flux_ref.shape
    slot_total = place_ref.shape[0]
    mean = sums_ref[...] / members
    flux = jnp.dot(mean, readout_ref[...], precision=HIGHEST, preferred_element_type=jnp.float32)
    col_iota = lax.broadcasted_iota(jnp.int32, (slot_total, tile_cols), 1)
    col_pick = (col_iota == place_ref[:, 1:2]).astype(jnp.float32)
    row_iota = lax.broadcasted_iota(jnp.int32, (tile_rows, slot_total), 0)
    row_pick = (row_iota == place_row_ref[0:1, :]) & (place_row_ref[4:5, :] > 0)
    for direction in range(2):
        pick = (row_pick & (place_row_ref[5:6, :] == direction)).astype(jnp.float32)
        hit_ref[direction] = jnp.dot(pick, col_pick, precision=HIGHEST, preferred_element_type=jnp.float32)
        for channel in range(channels):
            spread = col_pick * flux[:, channel : channel + 1]
            flux_ref[direction, channel] = jnp.dot(
                pick, spread, precision=HIGHEST, preferred_element_type=jnp.float32
            )


ANY = pl.BlockSpec(memory_space=pl.ANY)
VMEM = pl.BlockSpec(memory_space=pltpu.VMEM)
SMEM = pl.BlockSpec(memory_space=pltpu.SMEM)


def per_device(macro_state, face_list, owner, face_states, micro_weight, lift_weight, readout):
    channels, tile_rows, tile_cols = macro_state.shape
    slot_total = face_list.shape[2]
    members, state_width = face_states.shape[3:]
    gx_count, gy_count = lax.axis_size("gx"), lax.axis_size("gy")
    devices = gx_count * gy_count
    capacity = max(2, slot_total // devices)
    assert capacity * devices == slot_total and devices & (devices - 1) == 0
    order = partner_order(gx_count, gy_count)
    raw = order[:RAW]
    block = jax.ShapeDtypeStruct((capacity, members, state_width), jnp.bfloat16)
    whole = jax.ShapeDtypeStruct((devices, capacity, members, state_width), jnp.bfloat16)
    me = lax.axis_index("gx") * gy_count + lax.axis_index("gy")
    me_ref = me.astype(jnp.int32).reshape(1)
    states = face_states.reshape(slot_total, members, state_width)
    faces = face_list.reshape(slot_total)

    def exchanged(value, k):
        return lax.ppermute(value, ("gx", "gy"), [(source, source ^ k) for source in range(devices)])

    slots_smem = jax.ShapeDtypeStruct((slot_total,), jnp.int32)

    def gather_scratch(count):
        return [
            pltpu.VMEM((count, capacity, members, state_width), jnp.bfloat16),
            pltpu.SemaphoreType.DMA((count, capacity)),
            pltpu.SemaphoreType.DMA((count, capacity)),
        ]

    fields = jnp.transpose(macro_state, (0, 2, 1))
    raw_first, first_row, first_col = pl.pallas_call(
        functools.partial(first_kernel, capacity, raw[0]),
        out_shape=[
            block,
            jax.ShapeDtypeStruct((channels, tile_cols), jnp.float32),
            jax.ShapeDtypeStruct((channels, tile_rows), jnp.float32),
        ],
        in_specs=[SMEM, SMEM, ANY, ANY],
        out_specs=[ANY, VMEM, VMEM],
        scratch_shapes=[
            pltpu.SMEM((slot_total,), jnp.int32),
            pltpu.VMEM(fields.shape, jnp.float32),
            pltpu.SemaphoreType.DMA,
        ]
        + gather_scratch(1),
        name="first",
    )(me_ref, owner.reshape(slot_total), fields, states)
    owners, raw_first = lax.optimization_barrier((owner.reshape(slot_total), raw_first))
    next_row = passed_along(first_row, "gx", -1)
    next_col = passed_along(first_col, "gy", -1)
    raw_got = [exchanged(raw_first, raw[0])]
    table, ids, *raw_sent = pl.pallas_call(
        functools.partial(route_kernel, capacity, raw[1:]),
        out_shape=[slots_smem, slots_smem] + [block] * (RAW - 1),
        in_specs=[SMEM, SMEM, SMEM, ANY],
        out_specs=[SMEM, SMEM] + [ANY] * (RAW - 1),
        scratch_shapes=[pltpu.SMEM((devices,), jnp.int32)] + gather_scratch(RAW - 1),
        name="route",
    )(me_ref, owners, faces, states)
    for turn, k in enumerate(raw[1:]):
        raw_got.append(exchanged(raw_sent[turn], k))

    live = ids >= 0
    safe = jnp.where(live, ids, 0)
    direction = safe // (tile_rows * tile_cols)
    cell = safe % (tile_rows * tile_cols)
    left_row, left_col = cell // tile_cols, cell % tile_cols
    right_row, right_col = left_row + direction, left_col + 1 - direction
    place = [left_row, left_col, right_row, right_col, live.astype(jnp.int32), direction, cell, safe]
    place_rows = jnp.stack(place, axis=0)
    place_cols = jnp.stack(place, axis=1)

    force, alive, *raw_force = pl.pallas_call(
        functools.partial(forcing_kernel, capacity, raw),
        out_shape=[jax.ShapeDtypeStruct((slot_total, state_width), jnp.float32)] * 2
        + [jax.ShapeDtypeStruct((2 * capacity, state_width), jnp.float32)] * len(raw),
        in_specs=[VMEM] * 5,
        out_specs=[VMEM] * (2 + len(raw)),
        name="forcing",
    )(fields, next_row, next_col, place_cols, lift_weight)

    force_got = []
    for turn, k in enumerate(raw):
        force_got.append(exchanged(raw_force[turn], k))

    groups = partner_groups(order)
    sums, relaxed = {}, {}
    for partners in groups:
        kept = [k for k in partners if k not in raw]
        *blocks, part = pl.pallas_call(
            functools.partial(relax_kernel, capacity, partners, kept, 0),
            out_shape=[whole if k == 0 else block for k in kept]
            + [jax.ShapeDtypeStruct((len(partners) * capacity, state_width), jnp.float32)],
            in_specs=[SMEM, SMEM, ANY, VMEM, VMEM, VMEM],
            out_specs=[ANY] * len(kept) + [VMEM],
            scratch_shapes=[
                pltpu.VMEM((2, capacity, members, state_width), jnp.bfloat16),
                pltpu.VMEM((2, capacity, members, state_width), jnp.bfloat16),
                pltpu.SemaphoreType.DMA((2, capacity)),
                pltpu.SemaphoreType.DMA((2,)),
            ],
        )(me_ref, table, states, force, alive, micro_weight)
        table, part = lax.optimization_barrier((table, part))
        for k, value in zip(kept, blocks):
            relaxed[k] = value
        for turn, k in enumerate(partners):
            sums[k] = part[turn * capacity : (turn + 1) * capacity]
    all_sums = jnp.concatenate([sums[k] for k in range(devices)], axis=0)

    got = {}
    for k in order[RAW:]:
        got[k] = exchanged(relaxed[k], k)

    face_flux, hit = pl.pallas_call(
        functools.partial(flux_kernel, members),
        out_shape=[
            jax.ShapeDtypeStruct((2, channels, tile_rows, tile_cols), jnp.float32),
            jax.ShapeDtypeStruct((2, tile_rows, tile_cols), jnp.float32),
        ],
        in_specs=[VMEM] * 4,
        out_specs=[VMEM] * 2,
        name="flux",
    )(all_sums, readout, place_cols, place_rows)
    beyond_row = jnp.concatenate([macro_state[:, 1:, :], next_row[:, None, :]], axis=1)
    beyond_col = jnp.concatenate([macro_state[:, :, 1:], next_col[:, :, None]], axis=2)
    east_flux = jnp.where(hit[0] > 0.5, face_flux[0], diffusion * (macro_state - beyond_col))
    south_flux = jnp.where(hit[1] > 0.5, face_flux[1], diffusion * (macro_state - beyond_row))
    west_flux = passed_along(east_flux[:, :, -1], "gy", 1)
    north_flux = passed_along(south_flux[:, -1, :], "gx", 1)
    out = relaxed[0]
    for turn, k in enumerate(raw):
        out = pl.pallas_call(
            functools.partial(land_kernel, capacity),
            out_shape=whole,
            in_specs=[SMEM, VMEM, VMEM, VMEM, ANY],
            out_specs=ANY,
            scratch_shapes=[
                pltpu.VMEM((capacity, members, state_width), jnp.bfloat16),
                pltpu.SemaphoreType.DMA,
            ],
            input_output_aliases={4: 0},
        )(jnp.bitwise_xor(me_ref, k), raw_got[turn], force_got[turn], micro_weight, out)

    def put(out, partners):
        return pl.pallas_call(
            functools.partial(put_kernel, partners),
            out_shape=whole,
            in_specs=[SMEM] + [ANY] * (len(partners) + 1),
            out_specs=ANY,
            scratch_shapes=[
                pltpu.VMEM((len(partners), capacity, members, state_width), jnp.bfloat16),
                pltpu.SemaphoreType.DMA((len(partners),)),
                pltpu.SemaphoreType.DMA((len(partners),)),
            ],
            input_output_aliases={len(partners) + 1: 0},
        )(me_ref, *[got[k] for k in partners], out)

    landings = [order[i : i + GROUP] for i in range(RAW, devices - 1, GROUP)]
    for partners in landings[:-1]:
        out = put(out, partners)
    out, west_flux, north_flux = lax.optimization_barrier((out, west_flux, north_flux))
    macro_next = macro_state - time_step * (
        east_flux
        - jnp.concatenate([west_flux[:, :, None], east_flux[:, :, :-1]], axis=2)
        + south_flux
        - jnp.concatenate([north_flux[:, None, :], south_flux[:, :-1, :]], axis=1)
    )
    out, macro_next = lax.optimization_barrier((out, macro_next))
    out = put(out, landings[-1])
    return macro_next, out.reshape(1, 1, devices, capacity, members, state_width)


def solution(mesh):
    return jax.shard_map(
        per_device,
        mesh=mesh,
        in_specs=(
            P(None, "gx", "gy"),
            P("gx", "gy", None),
            P("gx", "gy", None, None),
            P("gx", "gy", None, None, None),
            P(),
            P(),
            P(),
        ),
        out_specs=(P(None, "gx", "gy"), P("gx", "gy", None, None, None, None)),
        check_vma=False,
    )
```

```python
import functools

import jax
import jax.numpy as jnp
from jax import lax
from jax.experimental import pallas as pl
from jax.experimental.pallas import tpu as pltpu
from jax.sharding import PartitionSpec as P


STEPS = 3
RAW = 2
GROUP = 4
LEAD = 4


diffusion = 0.2
relax_rate = 0.5
time_step = 0.5
HIGHEST = lax.Precision.HIGHEST


def passed_along(value, axis, steps):
    count = lax.axis_size(axis)
    pairs = [(source, (source + steps) % count) for source in range(count)]
    return lax.ppermute(value, axis, pairs)


def partner_order(gx_count, gy_count):
    devices = gx_count * gy_count
    far_bit, row_bit, col_bit = gy_count // 2, 1, devices // 2
    turns = lambda k: (bool(k & (far_bit // 2)), bool(k & row_bit), bool(k & col_bit), k)
    far = sorted([k for k in range(1, devices) if k & far_bit], key=turns)
    near = [k for k in range(1, devices) if not k & far_bit]
    near.sort(key=lambda k: (not k & row_bit, not k & col_bit, k))
    far.append(far.pop(len(far) // 2))
    order = far[:LEAD]
    for k in far[LEAD:-1]:
        order += near[:1] + [k]
        near = near[1:]
    return order + near + far[-1:]


def partner_groups(order):
    todo = order[RAW:] + order[:RAW] + [0]
    return [todo[:2]] + [todo[i : i + GROUP] for i in range(2, len(todo), GROUP)]


def block_copies(turns, capacity, slot_of, states_ref, out_refs, buffer, in_sem, out_sem):
    def fetch(turn, i):
        return pltpu.make_async_copy(states_ref.at[slot_of(turn, i)], buffer.at[turn, i], in_sem.at[turn, i])

    def send(turn, i):
        return pltpu.make_async_copy(buffer.at[turn, i], out_refs[turn].at[i], out_sem.at[turn, i])

    steps = [(turn, i) for turn in range(turns) for i in range(capacity)]
    for step in steps:
        fetch(*step).start()
    for step in steps:
        fetch(*step).wait()
        send(*step).start()
    for step in steps:
        send(*step).wait()


def first_kernel(capacity, partner, me_ref, owner_ref, macro_ref, states_ref, out_ref, row_ref, col_ref, *scratch):
    slot_ref, macro_buffer, macro_sem, in_sem = scratch
    slot_total = owner_ref.shape[0]
    owner = jnp.bitwise_xor(me_ref[0], partner)
    fields = pltpu.make_async_copy(macro_ref, macro_buffer, macro_sem)
    fields.start()

    def look(slot, found):
        slot_ref[found] = slot
        return found + (owner_ref[slot] == owner).astype(jnp.int32)

    lax.fori_loop(0, slot_total, look, jnp.int32(0), unroll=8)

    def fetch(i):
        return pltpu.make_async_copy(states_ref.at[slot_ref[i]], out_ref.at[i], in_sem.at[i])

    for i in range(capacity):
        fetch(i).start()
    fields.wait()
    channels, _, tile_rows = macro_buffer.shape
    pick = (lax.broadcasted_iota(jnp.int32, (8, tile_rows), 1) == 0).astype(jnp.float32)
    for channel in range(channels):
        field = macro_buffer[channel]
        col_ref[channel : channel + 1, :] = field[0:1, :]
        rows = lax.dot_general(
            pick, field, (((1,), (1,)), ((), ())), precision=HIGHEST, preferred_element_type=jnp.float32
        )
        row_ref[channel : channel + 1, :] = rows[0:1, :]
    for i in range(capacity):
        fetch(i).wait()


def route_kernel(capacity, partners, me_ref, owner_ref, face_ref, states_ref, table_ref, ids_ref, *rest):
    out_refs, (count_ref, buffer, in_sem, out_sem) = rest[: len(partners)], rest[len(partners) :]
    slot_total = owner_ref.shape[0]
    me = me_ref[0]

    def clear(number, carry):
        count_ref[number] = 0
        return carry

    lax.fori_loop(0, count_ref.shape[0], clear, 0)

    def place(slot, carry):
        code = jnp.bitwise_xor(owner_ref[slot], me)
        rank = count_ref[code]
        count_ref[code] = rank + 1
        position = code * capacity + rank
        table_ref[position] = slot
        ids_ref[position] = face_ref[slot]
        return carry

    lax.fori_loop(0, slot_total, place, 0, unroll=8)
    slot_of = lambda turn, i: table_ref[partners[turn] * capacity + i]
    block_copies(len(partners), capacity, slot_of, states_ref, out_refs, buffer, in_sem, out_sem)


def forcing_kernel(
    capacity, raw, macro_ref, row_ref, col_ref, place_ref, lift_ref, force_ref, live_ref, *out_refs
):
    channels, tile_cols, tile_rows = macro_ref.shape
    slot_total = place_ref.shape[0]
    place = place_ref[...]
    left_row, left_col, right_row, right_col, live = [place[:, i : i + 1] for i in range(5)]
    row_iota = lax.broadcasted_iota(jnp.int32, (slot_total, tile_rows), 1)
    col_iota = lax.broadcasted_iota(jnp.int32, (slot_total, tile_cols), 1)
    left_pick = (col_iota == left_col).astype(jnp.float32)
    right_pick = (col_iota == right_col).astype(jnp.float32)
    left_mask = row_iota == left_row
    right_mask = row_iota == right_row
    edge_row = (col_iota == right_col) & (right_row == tile_rows)
    edge_col = right_mask & (right_col == tile_cols)
    total = jnp.zeros((slot_total, lift_ref.shape[1]), jnp.float32)
    for channel in range(channels):
        block = macro_ref[channel]
        left = jnp.dot(left_pick, block, precision=HIGHEST, preferred_element_type=jnp.float32)
        left = jnp.sum(jnp.where(left_mask, left, 0.0), axis=1, keepdims=True)
        right = jnp.dot(right_pick, block, precision=HIGHEST, preferred_element_type=jnp.float32)
        right = jnp.where(right_mask, right, 0.0) + jnp.where(edge_col, col_ref[channel : channel + 1, :], 0.0)
        right = jnp.sum(right, axis=1, keepdims=True)
        beyond = jnp.where(edge_row, row_ref[channel : channel + 1, :], 0.0)
        right = right + jnp.sum(beyond, axis=1, keepdims=True)
        total = total + left * lift_ref[channel : channel + 1, :]
        total = total + right * lift_ref[channels + channel : channels + channel + 1, :]
    force_ref[...] = total
    alive = jnp.broadcast_to((live > 0).astype(jnp.float32), total.shape)
    live_ref[...] = alive
    for turn, k in enumerate(raw):
        out_refs[turn][0:capacity, :] = total[k * capacity : (k + 1) * capacity, :]
        out_refs[turn][capacity:, :] = alive[k * capacity : (k + 1) * capacity, :]


def relaxed_states(current, force, weight, live):
    slots, members, width = current.shape
    force = force.reshape(slots, 1, width)
    for _ in range(STEPS):
        activation = jnp.dot(current.reshape(slots * members, width), weight, preferred_element_type=jnp.float32)
        activation = activation.reshape(slots, members, width) + force
        current = (
            (1.0 - relax_rate) * current.astype(jnp.float32) + relax_rate * jnp.tanh(activation)
        ).astype(jnp.bfloat16)
    return current * live.astype(jnp.bfloat16).reshape(slots, 1, width)


def relax_kernel(
    capacity, partners, kept, own, me_ref, table_ref, states_ref, force_ref, live_ref, weight_ref, *rest
):
    out_refs, (sums_ref, in_buffer, out_buffer, in_sem, out_sem) = rest[: len(kept)], rest[len(kept) :]
    target = {k: ref for k, ref in zip(kept, out_refs)}

    def fetch(turn, i):
        slot = table_ref[partners[turn] * capacity + i]
        return pltpu.make_async_copy(states_ref.at[slot], in_buffer.at[turn % 2, i], in_sem.at[turn % 2, i])

    def send(turn):
        k = partners[turn]
        ref = target[k].at[me_ref[0]] if k == own else target[k]
        return pltpu.make_async_copy(out_buffer.at[turn % 2], ref, out_sem.at[turn % 2])

    for i in range(capacity):
        fetch(0, i).start()
    weight = weight_ref[...]
    waiting = {}
    for turn, k in enumerate(partners):
        if turn + 1 < len(partners):
            for i in range(capacity):
                fetch(turn + 1, i).start()
        if turn % 2 in waiting:
            send(waiting.pop(turn % 2)).wait()
        for i in range(capacity):
            fetch(turn, i).wait()

        rows = slice(k * capacity, (k + 1) * capacity)
        block = relaxed_states(in_buffer[turn % 2], force_ref[rows, :], weight, live_ref[rows, :])
        out_buffer[turn % 2] = block
        sums_ref[turn * capacity : (turn + 1) * capacity, :] = jnp.sum(block.astype(jnp.float32), axis=1)
        if k in target:
            send(turn).start()
            waiting[turn % 2] = turn
    for turn in waiting.values():
        send(turn).wait()


def land_kernel(capacity, source_ref, raw_ref, force_ref, weight_ref, whole_ref, out_ref, buffer, out_sem):
    buffer[...] = relaxed_states(
        raw_ref[...], force_ref[0:capacity, :], weight_ref[...], force_ref[capacity:, :]
    )
    copy = pltpu.make_async_copy(buffer, out_ref.at[source_ref[0]], out_sem)
    copy.start()
    copy.wait()


def put_kernel(partners, me_ref, *rest):
    got_refs, (_, out_ref, buffer, in_sem, out_sem) = rest[: len(partners)], rest[len(partners) :]
    places = [jnp.bitwise_xor(me_ref[0], k) for k in partners]
    fetches = [pltpu.make_async_copy(got_refs[i], buffer.at[i], in_sem.at[i]) for i in range(len(partners))]
    sends = [
        pltpu.make_async_copy(buffer.at[i], out_ref.at[place], out_sem.at[i]) for i, place in enumerate(places)
    ]
    for fetch in fetches:
        fetch.start()
    for fetch, send in zip(fetches, sends):
        fetch.wait()
        send.start()
    for send in sends:
        send.wait()


def flux_kernel(members, sums_ref, readout_ref, place_ref, place_row_ref, flux_ref, hit_ref):
    _, channels, tile_rows, tile_cols = flux_ref.shape
    slot_total = place_ref.shape[0]
    mean = sums_ref[...] / members
    flux = jnp.dot(mean, readout_ref[...], precision=HIGHEST, preferred_element_type=jnp.float32)
    col_iota = lax.broadcasted_iota(jnp.int32, (slot_total, tile_cols), 1)
    col_pick = (col_iota == place_ref[:, 1:2]).astype(jnp.float32)
    row_iota = lax.broadcasted_iota(jnp.int32, (tile_rows, slot_total), 0)
    row_pick = (row_iota == place_row_ref[0:1, :]) & (place_row_ref[4:5, :] > 0)
    for direction in range(2):
        pick = (row_pick & (place_row_ref[5:6, :] == direction)).astype(jnp.float32)
        hit_ref[direction] = jnp.dot(pick, col_pick, precision=HIGHEST, preferred_element_type=jnp.float32)
        for channel in range(channels):
            spread = col_pick * flux[:, channel : channel + 1]
            flux_ref[direction, channel] = jnp.dot(
                pick, spread, precision=HIGHEST, preferred_element_type=jnp.float32
            )


ANY = pl.BlockSpec(memory_space=pl.ANY)
VMEM = pl.BlockSpec(memory_space=pltpu.VMEM)
SMEM = pl.BlockSpec(memory_space=pltpu.SMEM)


def per_device(macro_state, face_list, owner, face_states, micro_weight, lift_weight, readout):
    channels, tile_rows, tile_cols = macro_state.shape
    slot_total = face_list.shape[2]
    members, state_width = face_states.shape[3:]
    gx_count, gy_count = lax.axis_size("gx"), lax.axis_size("gy")
    devices = gx_count * gy_count
    capacity = max(2, slot_total // devices)
    assert capacity * devices == slot_total and devices & (devices - 1) == 0
    order = partner_order(gx_count, gy_count)
    raw = order[:RAW]
    block = jax.ShapeDtypeStruct((capacity, members, state_width), jnp.bfloat16)
    whole = jax.ShapeDtypeStruct((devices, capacity, members, state_width), jnp.bfloat16)
    me = lax.axis_index("gx") * gy_count + lax.axis_index("gy")
    me_ref = me.astype(jnp.int32).reshape(1)
    states = face_states.reshape(slot_total, members, state_width)
    faces = face_list.reshape(slot_total)

    def exchanged(value, k):
        return lax.ppermute(value, ("gx", "gy"), [(source, source ^ k) for source in range(devices)])

    slots_smem = jax.ShapeDtypeStruct((slot_total,), jnp.int32)

    def gather_scratch(count):
        return [
            pltpu.VMEM((count, capacity, members, state_width), jnp.bfloat16),
            pltpu.SemaphoreType.DMA((count, capacity)),
            pltpu.SemaphoreType.DMA((count, capacity)),
        ]

    fields = jnp.transpose(macro_state, (0, 2, 1))
    raw_first, first_row, first_col = pl.pallas_call(
        functools.partial(first_kernel, capacity, raw[0]),
        out_shape=[
            pltpu.VMEM(block.shape, block.dtype),
            pltpu.VMEM((channels, tile_cols), jnp.float32),
            pltpu.VMEM((channels, tile_rows), jnp.float32),
        ],
        in_specs=[SMEM, SMEM, ANY, ANY],
        out_specs=[VMEM, VMEM, VMEM],
        scratch_shapes=[
            pltpu.SMEM((slot_total,), jnp.int32),
            pltpu.VMEM(fields.shape, jnp.float32),
            pltpu.SemaphoreType.DMA,
            pltpu.SemaphoreType.DMA((capacity,)),
        ],
        name="first",
    )(me_ref, owner.reshape(slot_total), fields, states)
    owners, raw_first = lax.optimization_barrier((owner.reshape(slot_total), raw_first))
    next_row = passed_along(first_row, "gx", -1)
    next_col = passed_along(first_col, "gy", -1)
    raw_got = [exchanged(raw_first, raw[0])]
    table, ids, *raw_sent = pl.pallas_call(
        functools.partial(route_kernel, capacity, raw[1:]),
        out_shape=[slots_smem, slots_smem] + [block] * (RAW - 1),
        in_specs=[SMEM, SMEM, SMEM, ANY],
        out_specs=[SMEM, SMEM] + [ANY] * (RAW - 1),
        scratch_shapes=[pltpu.SMEM((devices,), jnp.int32)] + gather_scratch(RAW - 1),
        name="route",
    )(me_ref, owners, faces, states)
    for turn, k in enumerate(raw[1:]):
        raw_got.append(exchanged(raw_sent[turn], k))

    live = ids >= 0
    safe = jnp.where(live, ids, 0)
    direction = safe // (tile_rows * tile_cols)
    cell = safe % (tile_rows * tile_cols)
    left_row, left_col = cell // tile_cols, cell % tile_cols
    right_row, right_col = left_row + direction, left_col + 1 - direction
    place = [left_row, left_col, right_row, right_col, live.astype(jnp.int32), direction, cell, safe]
    place_rows = jnp.stack(place, axis=0)
    place_cols = jnp.stack(place, axis=1)

    force, alive, *raw_force = pl.pallas_call(
        functools.partial(forcing_kernel, capacity, raw),
        out_shape=[jax.ShapeDtypeStruct((slot_total, state_width), jnp.float32)] * 2
        + [jax.ShapeDtypeStruct((2 * capacity, state_width), jnp.float32)] * len(raw),
        in_specs=[VMEM] * 5,
        out_specs=[VMEM] * (2 + len(raw)),
        name="forcing",
    )(fields, next_row, next_col, place_cols, lift_weight)

    force_got = []
    for turn, k in enumerate(raw):
        force_got.append(exchanged(raw_force[turn], k))

    groups = partner_groups(order)
    sums, relaxed = {}, {}
    for partners in groups:
        kept = [k for k in partners if k not in raw]
        *blocks, part = pl.pallas_call(
            functools.partial(relax_kernel, capacity, partners, kept, 0),
            out_shape=[whole if k == 0 else block for k in kept]
            + [jax.ShapeDtypeStruct((len(partners) * capacity, state_width), jnp.float32)],
            in_specs=[SMEM, SMEM, ANY, VMEM, VMEM, VMEM],
            out_specs=[ANY] * len(kept) + [VMEM],
            scratch_shapes=[
                pltpu.VMEM((2, capacity, members, state_width), jnp.bfloat16),
                pltpu.VMEM((2, capacity, members, state_width), jnp.bfloat16),
                pltpu.SemaphoreType.DMA((2, capacity)),
                pltpu.SemaphoreType.DMA((2,)),
            ],
        )(me_ref, table, states, force, alive, micro_weight)
        table, part = lax.optimization_barrier((table, part))
        for k, value in zip(kept, blocks):
            relaxed[k] = value
        for turn, k in enumerate(partners):
            sums[k] = part[turn * capacity : (turn + 1) * capacity]
    all_sums = jnp.concatenate([sums[k] for k in range(devices)], axis=0)

    got = {}
    for k in order[RAW:]:
        got[k] = exchanged(relaxed[k], k)

    face_flux, hit = pl.pallas_call(
        functools.partial(flux_kernel, members),
        out_shape=[
            jax.ShapeDtypeStruct((2, channels, tile_rows, tile_cols), jnp.float32),
            jax.ShapeDtypeStruct((2, tile_rows, tile_cols), jnp.float32),
        ],
        in_specs=[VMEM] * 4,
        out_specs=[VMEM] * 2,
        name="flux",
    )(all_sums, readout, place_cols, place_rows)
    beyond_row = jnp.concatenate([macro_state[:, 1:, :], next_row[:, None, :]], axis=1)
    beyond_col = jnp.concatenate([macro_state[:, :, 1:], next_col[:, :, None]], axis=2)
    east_flux = jnp.where(hit[0] > 0.5, face_flux[0], diffusion * (macro_state - beyond_col))
    south_flux = jnp.where(hit[1] > 0.5, face_flux[1], diffusion * (macro_state - beyond_row))
    west_flux = passed_along(east_flux[:, :, -1], "gy", 1)
    north_flux = passed_along(south_flux[:, -1, :], "gx", 1)
    out = relaxed[0]
    for turn, k in enumerate(raw):
        out = pl.pallas_call(
            functools.partial(land_kernel, capacity),
            out_shape=whole,
            in_specs=[SMEM, VMEM, VMEM, VMEM, ANY],
            out_specs=ANY,
            scratch_shapes=[
                pltpu.VMEM((capacity, members, state_width), jnp.bfloat16),
                pltpu.SemaphoreType.DMA,
            ],
            input_output_aliases={4: 0},
        )(jnp.bitwise_xor(me_ref, k), raw_got[turn], force_got[turn], micro_weight, out)

    def put(out, partners):
        return pl.pallas_call(
            functools.partial(put_kernel, partners),
            out_shape=whole,
            in_specs=[SMEM] + [ANY] * (len(partners) + 1),
            out_specs=ANY,
            scratch_shapes=[
                pltpu.VMEM((len(partners), capacity, members, state_width), jnp.bfloat16),
                pltpu.SemaphoreType.DMA((len(partners),)),
                pltpu.SemaphoreType.DMA((len(partners),)),
            ],
            input_output_aliases={len(partners) + 1: 0},
        )(me_ref, *[got[k] for k in partners], out)

    waiting = order[RAW:-1]
    head = len(waiting) % GROUP
    landings = [waiting[:head]] if head else []
    landings += [waiting[i : i + GROUP] for i in range(head, len(waiting), GROUP)]
    for partners in landings:
        out = put(out, partners)
    out, west_flux, north_flux = lax.optimization_barrier((out, west_flux, north_flux))
    macro_next = macro_state - time_step * (
        east_flux
        - jnp.concatenate([west_flux[:, :, None], east_flux[:, :, :-1]], axis=2)
        + south_flux
        - jnp.concatenate([north_flux[:, None, :], south_flux[:, :-1, :]], axis=1)
    )
    out, macro_next = lax.optimization_barrier((out, jnp.transpose(macro_next, (0, 2, 1))))
    macro_next = jnp.transpose(macro_next, (0, 2, 1))
    last = order[-1]
    out = lax.dynamic_update_slice(out, got[last][None], (jnp.bitwise_xor(me, last), 0, 0, 0))
    return macro_next, out.reshape(1, 1, devices, capacity, members, state_width)


def solution(mesh):
    return jax.shard_map(
        per_device,
        mesh=mesh,
        in_specs=(
            P(None, "gx", "gy"),
            P("gx", "gy", None),
            P("gx", "gy", None, None),
            P("gx", "gy", None, None, None),
            P(),
            P(),
            P(),
        ),
        out_specs=(P(None, "gx", "gy"), P("gx", "gy", None, None, None, None)),
        check_vma=False,
    )
```

```python
import functools

import jax
import jax.numpy as jnp
from jax import lax
from jax.experimental import pallas as pl
from jax.experimental.pallas import tpu as pltpu
from jax.sharding import PartitionSpec as P


STEPS = 3
RAW = 2
GROUP = 4
LEAD = 6


diffusion = 0.2
relax_rate = 0.5
time_step = 0.5
HIGHEST = lax.Precision.HIGHEST


def passed_along(value, axis, steps):
    count = lax.axis_size(axis)
    pairs = [(source, (source + steps) % count) for source in range(count)]
    return lax.ppermute(value, axis, pairs)


def partner_order(gx_count, gy_count):
    devices = gx_count * gy_count
    far_bit, row_bit, col_bit = gy_count // 2, 1, devices // 2
    turns = lambda k: (bool(k & (far_bit // 2)), bool(k & row_bit), bool(k & col_bit), k)
    far = sorted([k for k in range(1, devices) if k & far_bit], key=turns)
    near = [k for k in range(1, devices) if not k & far_bit]
    near.sort(key=lambda k: (not k & row_bit, not k & col_bit, k))
    quarter = len(far) // 4
    far[quarter : 2 * quarter] = far[quarter : 2 * quarter][::-1]
    far.append(far.pop(len(far) // 2))
    order = far[:LEAD]
    for k in far[LEAD:-1]:
        order += near[:1] + [k]
        near = near[1:]
    return order + near + far[-1:]


def partner_groups(order):
    todo = order[RAW:] + order[:RAW] + [0]
    return [todo[:2]] + [todo[i : i + GROUP] for i in range(2, len(todo), GROUP)]


def block_copies(turns, capacity, slot_of, states_ref, out_refs, buffer, in_sem, out_sem):
    def fetch(turn, i):
        return pltpu.make_async_copy(states_ref.at[slot_of(turn, i)], buffer.at[turn, i], in_sem.at[turn, i])

    def send(turn, i):
        return pltpu.make_async_copy(buffer.at[turn, i], out_refs[turn].at[i], out_sem.at[turn, i])

    steps = [(turn, i) for turn in range(turns) for i in range(capacity)]
    for step in steps:
        fetch(*step).start()
    for step in steps:
        fetch(*step).wait()
        send(*step).start()
    for step in steps:
        send(*step).wait()


def first_kernel(capacity, partner, owner_ref, macro_ref, states_ref, out_ref, row_ref, col_ref, *scratch):
    slot_ref, macro_buffer, macro_sem, in_sem = scratch
    slot_total = owner_ref.shape[0]
    me = lax.axis_index("gx") * lax.axis_size("gy") + lax.axis_index("gy")
    owner = jnp.bitwise_xor(me.astype(jnp.int32), partner)
    fields = pltpu.make_async_copy(macro_ref, macro_buffer, macro_sem)
    fields.start()

    def look(slot, found):
        slot_ref[found] = slot
        return found + (owner_ref[slot] == owner).astype(jnp.int32)

    lax.fori_loop(0, slot_total, look, jnp.int32(0), unroll=8)

    def fetch(i):
        return pltpu.make_async_copy(states_ref.at[slot_ref[i]], out_ref.at[i], in_sem.at[i])

    for i in range(capacity):
        fetch(i).start()
    fields.wait()
    channels, _, tile_rows = macro_buffer.shape
    pick = (lax.broadcasted_iota(jnp.int32, (8, tile_rows), 1) == 0).astype(jnp.float32)
    for channel in range(channels):
        field = macro_buffer[channel]
        col_ref[channel : channel + 1, :] = field[0:1, :]
        rows = lax.dot_general(
            pick, field, (((1,), (1,)), ((), ())), precision=HIGHEST, preferred_element_type=jnp.float32
        )
        row_ref[channel : channel + 1, :] = rows[0:1, :]
    for i in range(capacity):
        fetch(i).wait()


def route_kernel(capacity, partners, me_ref, owner_ref, face_ref, states_ref, table_ref, ids_ref, *rest):
    out_refs, (count_ref, buffer, in_sem, out_sem) = rest[: len(partners)], rest[len(partners) :]
    slot_total = owner_ref.shape[0]
    me = me_ref[0]

    def clear(number, carry):
        count_ref[number] = 0
        return carry

    lax.fori_loop(0, count_ref.shape[0], clear, 0)

    def place(slot, carry):
        code = jnp.bitwise_xor(owner_ref[slot], me)
        rank = count_ref[code]
        count_ref[code] = rank + 1
        position = code * capacity + rank
        table_ref[position] = slot
        ids_ref[position] = face_ref[slot]
        return carry

    lax.fori_loop(0, slot_total, place, 0, unroll=8)
    slot_of = lambda turn, i: table_ref[partners[turn] * capacity + i]
    block_copies(len(partners), capacity, slot_of, states_ref, out_refs, buffer, in_sem, out_sem)


def forcing_kernel(
    capacity, raw, macro_ref, row_ref, col_ref, place_ref, lift_ref, force_ref, live_ref, *out_refs
):
    channels, tile_cols, tile_rows = macro_ref.shape
    slot_total = place_ref.shape[0]
    place = place_ref[...]
    left_row, left_col, right_row, right_col, live = [place[:, i : i + 1] for i in range(5)]
    row_iota = lax.broadcasted_iota(jnp.int32, (slot_total, tile_rows), 1)
    col_iota = lax.broadcasted_iota(jnp.int32, (slot_total, tile_cols), 1)
    left_pick = (col_iota == left_col).astype(jnp.float32)
    right_pick = (col_iota == right_col).astype(jnp.float32)
    left_mask = row_iota == left_row
    right_mask = row_iota == right_row
    edge_row = (col_iota == right_col) & (right_row == tile_rows)
    edge_col = right_mask & (right_col == tile_cols)
    total = jnp.zeros((slot_total, lift_ref.shape[1]), jnp.float32)
    for channel in range(channels):
        block = macro_ref[channel]
        left = jnp.dot(left_pick, block, precision=HIGHEST, preferred_element_type=jnp.float32)
        left = jnp.sum(jnp.where(left_mask, left, 0.0), axis=1, keepdims=True)
        right = jnp.dot(right_pick, block, precision=HIGHEST, preferred_element_type=jnp.float32)
        right = jnp.where(right_mask, right, 0.0) + jnp.where(edge_col, col_ref[channel : channel + 1, :], 0.0)
        right = jnp.sum(right, axis=1, keepdims=True)
        beyond = jnp.where(edge_row, row_ref[channel : channel + 1, :], 0.0)
        right = right + jnp.sum(beyond, axis=1, keepdims=True)
        total = total + left * lift_ref[channel : channel + 1, :]
        total = total + right * lift_ref[channels + channel : channels + channel + 1, :]
    force_ref[...] = total
    alive = jnp.broadcast_to((live > 0).astype(jnp.float32), total.shape)
    live_ref[...] = alive
    for turn, k in enumerate(raw):
        out_refs[turn][0:capacity, :] = total[k * capacity : (k + 1) * capacity, :]
        out_refs[turn][capacity:, :] = alive[k * capacity : (k + 1) * capacity, :]


def relaxed_states(current, force, weight, live):
    slots, members, width = current.shape
    force = force.reshape(slots, 1, width)
    for _ in range(STEPS):
        activation = jnp.dot(current.reshape(slots * members, width), weight, preferred_element_type=jnp.float32)
        activation = activation.reshape(slots, members, width) + force
        current = (
            (1.0 - relax_rate) * current.astype(jnp.float32) + relax_rate * jnp.tanh(activation)
        ).astype(jnp.bfloat16)
    return current * live.astype(jnp.bfloat16).reshape(slots, 1, width)


def relax_kernel(
    capacity, partners, kept, own, me_ref, table_ref, states_ref, force_ref, live_ref, weight_ref, *rest
):
    out_refs, (sums_ref, in_buffer, out_buffer, in_sem, out_sem) = rest[: len(kept)], rest[len(kept) :]
    target = {k: ref for k, ref in zip(kept, out_refs)}

    def fetch(turn, i):
        slot = table_ref[partners[turn] * capacity + i]
        return pltpu.make_async_copy(states_ref.at[slot], in_buffer.at[turn % 2, i], in_sem.at[turn % 2, i])

    def send(turn):
        k = partners[turn]
        ref = target[k].at[me_ref[0]] if k == own else target[k]
        return pltpu.make_async_copy(out_buffer.at[turn % 2], ref, out_sem.at[turn % 2])

    for i in range(capacity):
        fetch(0, i).start()
    weight = weight_ref[...]
    waiting = {}
    for turn, k in enumerate(partners):
        if turn + 1 < len(partners):
            for i in range(capacity):
                fetch(turn + 1, i).start()
        if turn % 2 in waiting:
            send(waiting.pop(turn % 2)).wait()
        for i in range(capacity):
            fetch(turn, i).wait()

        rows = slice(k * capacity, (k + 1) * capacity)
        block = relaxed_states(in_buffer[turn % 2], force_ref[rows, :], weight, live_ref[rows, :])
        out_buffer[turn % 2] = block
        sums_ref[turn * capacity : (turn + 1) * capacity, :] = jnp.sum(block.astype(jnp.float32), axis=1)
        if k in target:
            send(turn).start()
            waiting[turn % 2] = turn
    for turn in waiting.values():
        send(turn).wait()


def land_kernel(capacity, source_ref, raw_ref, force_ref, weight_ref, whole_ref, out_ref, buffer, out_sem):
    buffer[...] = relaxed_states(
        raw_ref[...], force_ref[0:capacity, :], weight_ref[...], force_ref[capacity:, :]
    )
    copy = pltpu.make_async_copy(buffer, out_ref.at[source_ref[0]], out_sem)
    copy.start()
    copy.wait()


def put_kernel(partners, me_ref, *rest):
    got_refs, (_, out_ref, buffer, in_sem, out_sem) = rest[: len(partners)], rest[len(partners) :]
    places = [jnp.bitwise_xor(me_ref[0], k) for k in partners]
    fetches = [pltpu.make_async_copy(got_refs[i], buffer.at[i], in_sem.at[i]) for i in range(len(partners))]
    sends = [
        pltpu.make_async_copy(buffer.at[i], out_ref.at[place], out_sem.at[i]) for i, place in enumerate(places)
    ]
    for fetch in fetches:
        fetch.start()
    for fetch, send in zip(fetches, sends):
        fetch.wait()
        send.start()
    for send in sends:
        send.wait()


def flux_kernel(members, sums_ref, readout_ref, place_ref, place_row_ref, flux_ref, hit_ref):
    _, channels, tile_rows, tile_cols = flux_ref.shape
    slot_total = place_ref.shape[0]
    mean = sums_ref[...] / members
    flux = jnp.dot(mean, readout_ref[...], precision=HIGHEST, preferred_element_type=jnp.float32)
    col_iota = lax.broadcasted_iota(jnp.int32, (slot_total, tile_cols), 1)
    col_pick = (col_iota == place_ref[:, 1:2]).astype(jnp.float32)
    row_iota = lax.broadcasted_iota(jnp.int32, (tile_rows, slot_total), 0)
    row_pick = (row_iota == place_row_ref[0:1, :]) & (place_row_ref[4:5, :] > 0)
    for direction in range(2):
        pick = (row_pick & (place_row_ref[5:6, :] == direction)).astype(jnp.float32)
        hit_ref[direction] = jnp.dot(pick, col_pick, precision=HIGHEST, preferred_element_type=jnp.float32)
        for channel in range(channels):
            spread = col_pick * flux[:, channel : channel + 1]
            flux_ref[direction, channel] = jnp.dot(
                pick, spread, precision=HIGHEST, preferred_element_type=jnp.float32
            )


ANY = pl.BlockSpec(memory_space=pl.ANY)
VMEM = pl.BlockSpec(memory_space=pltpu.VMEM)
SMEM = pl.BlockSpec(memory_space=pltpu.SMEM)


def per_device(macro_state, face_list, owner, face_states, micro_weight, lift_weight, readout):
    channels, tile_rows, tile_cols = macro_state.shape
    slot_total = face_list.shape[2]
    members, state_width = face_states.shape[3:]
    gx_count, gy_count = lax.axis_size("gx"), lax.axis_size("gy")
    devices = gx_count * gy_count
    capacity = max(2, slot_total // devices)
    assert capacity * devices == slot_total and devices & (devices - 1) == 0
    order = partner_order(gx_count, gy_count)
    raw = order[:RAW]
    block = jax.ShapeDtypeStruct((capacity, members, state_width), jnp.bfloat16)
    whole = jax.ShapeDtypeStruct((devices, capacity, members, state_width), jnp.bfloat16)
    me = lax.axis_index("gx") * gy_count + lax.axis_index("gy")
    me_ref = me.astype(jnp.int32).reshape(1)
    states = face_states.reshape(slot_total, members, state_width)
    faces = face_list.reshape(slot_total)

    def exchanged(value, k):
        return lax.ppermute(value, ("gx", "gy"), [(source, source ^ k) for source in range(devices)])

    slots_smem = jax.ShapeDtypeStruct((slot_total,), jnp.int32)

    def gather_scratch(count):
        return [
            pltpu.VMEM((count, capacity, members, state_width), jnp.bfloat16),
            pltpu.SemaphoreType.DMA((count, capacity)),
            pltpu.SemaphoreType.DMA((count, capacity)),
        ]

    fields = jnp.transpose(macro_state, (0, 2, 1))
    raw_first, first_row, first_col = pl.pallas_call(
        functools.partial(first_kernel, capacity, raw[0]),
        out_shape=[
            pltpu.VMEM(block.shape, block.dtype),
            pltpu.VMEM((channels, tile_cols), jnp.float32),
            pltpu.VMEM((channels, tile_rows), jnp.float32),
        ],
        in_specs=[SMEM, ANY, ANY],
        out_specs=[VMEM, VMEM, VMEM],
        scratch_shapes=[
            pltpu.SMEM((slot_total,), jnp.int32),
            pltpu.VMEM(fields.shape, jnp.float32),
            pltpu.SemaphoreType.DMA,
            pltpu.SemaphoreType.DMA((capacity,)),
        ],
        name="first",
    )(owner.reshape(slot_total), fields, states)
    owners, raw_first = lax.optimization_barrier((owner.reshape(slot_total), raw_first))
    next_row = passed_along(first_row, "gx", -1)
    next_col = passed_along(first_col, "gy", -1)
    raw_got = [exchanged(raw_first, raw[0])]
    table, ids, *raw_sent = pl.pallas_call(
        functools.partial(route_kernel, capacity, raw[1:]),
        out_shape=[slots_smem, slots_smem] + [block] * (RAW - 1),
        in_specs=[SMEM, SMEM, SMEM, ANY],
        out_specs=[SMEM, SMEM] + [ANY] * (RAW - 1),
        scratch_shapes=[pltpu.SMEM((devices,), jnp.int32)] + gather_scratch(RAW - 1),
        name="route",
    )(me_ref, owners, faces, states)
    for turn, k in enumerate(raw[1:]):
        raw_got.append(exchanged(raw_sent[turn], k))

    live = ids >= 0
    safe = jnp.where(live, ids, 0)
    direction = safe // (tile_rows * tile_cols)
    cell = safe % (tile_rows * tile_cols)
    left_row, left_col = cell // tile_cols, cell % tile_cols
    right_row, right_col = left_row + direction, left_col + 1 - direction
    place = [left_row, left_col, right_row, right_col, live.astype(jnp.int32), direction, cell, safe]
    place_rows = jnp.stack(place, axis=0)
    place_cols = jnp.stack(place, axis=1)

    force, alive, *raw_force = pl.pallas_call(
        functools.partial(forcing_kernel, capacity, raw),
        out_shape=[jax.ShapeDtypeStruct((slot_total, state_width), jnp.float32)] * 2
        + [jax.ShapeDtypeStruct((2 * capacity, state_width), jnp.float32)] * len(raw),
        in_specs=[VMEM] * 5,
        out_specs=[VMEM] * (2 + len(raw)),
        name="forcing",
    )(fields, next_row, next_col, place_cols, lift_weight)

    force_got = []
    for turn, k in enumerate(raw):
        force_got.append(exchanged(raw_force[turn], k))

    groups = partner_groups(order)
    sums, relaxed = {}, {}
    for partners in groups:
        kept = [k for k in partners if k not in raw]
        *blocks, part = pl.pallas_call(
            functools.partial(relax_kernel, capacity, partners, kept, 0),
            out_shape=[whole if k == 0 else block for k in kept]
            + [jax.ShapeDtypeStruct((len(partners) * capacity, state_width), jnp.float32)],
            in_specs=[SMEM, SMEM, ANY, VMEM, VMEM, VMEM],
            out_specs=[ANY] * len(kept) + [VMEM],
            scratch_shapes=[
                pltpu.VMEM((2, capacity, members, state_width), jnp.bfloat16),
                pltpu.VMEM((2, capacity, members, state_width), jnp.bfloat16),
                pltpu.SemaphoreType.DMA((2, capacity)),
                pltpu.SemaphoreType.DMA((2,)),
            ],
        )(me_ref, table, states, force, alive, micro_weight)
        table, part = lax.optimization_barrier((table, part))
        for k, value in zip(kept, blocks):
            relaxed[k] = value
        for turn, k in enumerate(partners):
            sums[k] = part[turn * capacity : (turn + 1) * capacity]
    all_sums = jnp.concatenate([sums[k] for k in range(devices)], axis=0)

    got = {}
    for k in order[RAW:]:
        got[k] = exchanged(relaxed[k], k)

    face_flux, hit = pl.pallas_call(
        functools.partial(flux_kernel, members),
        out_shape=[
            jax.ShapeDtypeStruct((2, channels, tile_rows, tile_cols), jnp.float32),
            jax.ShapeDtypeStruct((2, tile_rows, tile_cols), jnp.float32),
        ],
        in_specs=[VMEM] * 4,
        out_specs=[VMEM] * 2,
        name="flux",
    )(all_sums, readout, place_cols, place_rows)
    beyond_row = jnp.concatenate([macro_state[:, 1:, :], next_row[:, None, :]], axis=1)
    beyond_col = jnp.concatenate([macro_state[:, :, 1:], next_col[:, :, None]], axis=2)
    east_flux = jnp.where(hit[0] > 0.5, face_flux[0], diffusion * (macro_state - beyond_col))
    south_flux = jnp.where(hit[1] > 0.5, face_flux[1], diffusion * (macro_state - beyond_row))
    west_flux = passed_along(east_flux[:, :, -1], "gy", 1)
    north_flux = passed_along(south_flux[:, -1, :], "gx", 1)
    out = relaxed[0]
    for turn, k in enumerate(raw):
        out = pl.pallas_call(
            functools.partial(land_kernel, capacity),
            out_shape=whole,
            in_specs=[SMEM, VMEM, VMEM, VMEM, ANY],
            out_specs=ANY,
            scratch_shapes=[
                pltpu.VMEM((capacity, members, state_width), jnp.bfloat16),
                pltpu.SemaphoreType.DMA,
            ],
            input_output_aliases={4: 0},
        )(jnp.bitwise_xor(me_ref, k), raw_got[turn], force_got[turn], micro_weight, out)

    def put(out, partners):
        return pl.pallas_call(
            functools.partial(put_kernel, partners),
            out_shape=whole,
            in_specs=[SMEM] + [ANY] * (len(partners) + 1),
            out_specs=ANY,
            scratch_shapes=[
                pltpu.VMEM((len(partners), capacity, members, state_width), jnp.bfloat16),
                pltpu.SemaphoreType.DMA((len(partners),)),
                pltpu.SemaphoreType.DMA((len(partners),)),
            ],
            input_output_aliases={len(partners) + 1: 0},
        )(me_ref, *[got[k] for k in partners], out)

    waiting = order[RAW:-1]
    head = len(waiting) % GROUP
    landings = [waiting[:head]] if head else []
    landings += [waiting[i : i + GROUP] for i in range(head, len(waiting), GROUP)]
    for partners in landings:
        out = put(out, partners)
    out, west_flux, north_flux = lax.optimization_barrier((out, west_flux, north_flux))
    macro_next = macro_state - time_step * (
        east_flux
        - jnp.concatenate([west_flux[:, :, None], east_flux[:, :, :-1]], axis=2)
        + south_flux
        - jnp.concatenate([north_flux[:, None, :], south_flux[:, :-1, :]], axis=1)
    )
    out, macro_next = lax.optimization_barrier((out, jnp.transpose(macro_next, (0, 2, 1))))
    macro_next = jnp.transpose(macro_next, (0, 2, 1))
    last = order[-1]
    out = lax.dynamic_update_slice(out, got[last][None], (jnp.bitwise_xor(me, last), 0, 0, 0))
    return macro_next, out.reshape(1, 1, devices, capacity, members, state_width)


def solution(mesh):
    return jax.shard_map(
        per_device,
        mesh=mesh,
        in_specs=(
            P(None, "gx", "gy"),
            P("gx", "gy", None),
            P("gx", "gy", None, None),
            P("gx", "gy", None, None, None),
            P(),
            P(),
            P(),
        ),
        out_specs=(P(None, "gx", "gy"), P("gx", "gy", None, None, None, None)),
        check_vma=False,
    )
```
